32 devices in a mesh: seq: 8 (over z, x), dp: 4 (over y, core).
Axes of the slice: x: 2, y: 2, z: 4, core: 2. Of those that a mesh axis runs over, the one named last changes fastest.
Arguments:
- queries: bfloat16 [4, 2048, 1536], P('dp', 'seq'), may hold values from -6 to 6
- key_vectors: bfloat16 [4, 2048, 1536], P('dp', 'seq'), may hold values from -6 to 6
- value_vectors: bfloat16 [4, 2048, 1536], P('dp', 'seq'), may hold values from -6 to 6
- features: bfloat16 [4, 2048, 2048], P('dp', 'seq'), may hold values from -6 to 6
- w_level: bfloat16 [2048, 144], replicated, may hold values from -0.125 to 0.125
- offsets: int32 [4, 16], P('dp', 'seq'), may hold values from 0 to 128, as said below
- cotangent: bfloat16 [4, 2048, 1536], P('dp', 'seq'), may hold values from -6 to 6
- final_grad: bfloat16 [4, 12, 128, 128], P('dp'), may hold values from -6 to 6
Outputs:
- normed: bfloat16 [4, 2048, 1536], P('dp', 'seq')
- grad_query: bfloat16 [4, 2048, 1536], P('dp', 'seq')
- grad_key: bfloat16 [4, 2048, 1536], P('dp', 'seq')
- grad_value: bfloat16 [4, 2048, 1536], P('dp', 'seq')
- grad_level: float32 [2048, 144], P('seq')
- final_state: float32 [4, 12, 128, 128], P('dp')
The draws below stay inside these ranges and needn't reach their ends.
Inputs may be any that keep to these rules, and one draw needn't show every extreme that they name: `offsets`: each stretch of 128 positions holds at most one document start, at the given place; the value 128 means that none starts in the stretch.
All inputs are finite; a program needn't handle non-finite values.
Results may differ from the reference program's by a relative error of at most 0.001.
Values sent between devices are 32-bit elements; how exact they have to be, the bound alone decides.
A program may use at most 128 MiB of HBM per device.

```python
import jax
import jax.numpy as jnp
from jax import lax

D = 2048
HEADS = 12
HEAD_DIM = 128
STRETCH = 128
LEVELS = 12
BATCH = 4
NCH = 16
SEQLEN = 2048


def draw_offsets(key, part):
    first_key, second_key = jax.random.split(jax.random.fold_in(key, 17))
    places = jax.random.randint(first_key, (BATCH, NCH), 0, STRETCH, dtype=jnp.int32)
    picked = jax.random.randint(second_key, (BATCH, NCH), 0, 10, dtype=jnp.int32) == 0
    return jnp.where(picked, places, STRETCH).astype(jnp.int32)


def with_spikes(values, stream_key, source, target, shards_of, factor):
    def block_of(dim):
        return (jnp.arange(values.shape[dim]) // (values.shape[dim] // shards_of)).reshape((-1,) + (1,) * (values.ndim - 1 - dim))

    one_side = jax.random.permutation(stream_key, shards_of)[block_of(target)]
    far = (block_of(target) + shards_of // 2) % shards_of
    return jnp.where((block_of(source) == one_side) | (block_of(source) == far), factor * values, values)


def steps_of(key, dims, shards, least, high):
    def one(dim, shards_of):
        draws = jax.random.uniform(jax.random.fold_in(jax.random.fold_in(key, 6), dim), (shards_of,), jnp.float32, least / len(shards), high / len(shards))
        return jnp.repeat(jnp.exp(draws), dims[dim] // shards_of).reshape((-1,) + (1,) * (len(dims) - dim - 1))

    factor_of = one(*shards[0])
    for cut in shards[1:]:
        factor_of = factor_of * one(*cut)
    return factor_of


def scatter_about(stream_key, shape, scale, reach, cuts=(), kind=jnp.bfloat16):
    result = scale * jax.random.normal(stream_key, shape, jnp.float32)
    if cuts:
        result = result * steps_of(stream_key, shape, cuts, -0.22, 0.18)
    return jnp.clip(result, -reach, reach).astype(kind)


def noise_with(rng, shape, spread, most, pieces, heavy, kind=jnp.bfloat16):
    drawn = spread * jax.random.normal(rng, shape, jnp.float32)
    if pieces:
        drawn = drawn * steps_of(rng, shape, pieces, -0.22, 0.18)
    return jnp.clip(with_spikes(drawn, jax.random.fold_in(rng, 3), *heavy), -most, most).astype(kind)


def setup_inputs(seed: int = 0) -> dict:
    key_list = jax.random.split(jax.random.key(seed), 9)
    return {
        "queries": scatter_about(key_list[0], (BATCH, SEQLEN, HEADS * HEAD_DIM), 1.0, 6.0, ((0, 4), (1, 8))),
        "key_vectors": scatter_about(key_list[1], (BATCH, SEQLEN, HEADS * HEAD_DIM), 1.0, 6.0, ((0, 4), (1, 8))),
        "value_vectors": scatter_about(key_list[2], (BATCH, SEQLEN, HEADS * HEAD_DIM), 1.0, 6.0, ((0, 4), (1, 8))),
        "features": noise_with(key_list[3], (BATCH, SEQLEN, D), 1.0, 6.0, ((0, 4), (1, 8)), (1, 2, 8, 2.0)),
        "w_level": scatter_about(key_list[4], (D, LEVELS * HEADS), D ** -0.5, 0.125),
        "offsets": draw_offsets(jax.random.fold_in(key_list[8], 71), 0),
        "cotangent": scatter_about(key_list[6], (BATCH, SEQLEN, HEADS * HEAD_DIM), 1.0, 6.0, ((0, 4), (1, 8))),
        "final_grad": scatter_about(key_list[7], (BATCH, HEADS, HEAD_DIM, HEAD_DIM), 1.0, 6.0, ((0, 4),)),
    }


highest = lax.Precision.HIGHEST
epsilon = 1e-06
state_scale = 0.0625

def normalize(summed):
    return summed * lax.rsqrt(lax.optimization_barrier(jnp.mean(summed * summed, -1, keepdims=True)) + epsilon)

def sequence_forward(query_f, key_f, value_f, level_gate, offsets):
    shaped = (NCH, STRETCH, HEADS, HEAD_DIM)
    query_c = query_f.reshape(shaped)
    key_c = key_f.reshape(shaped)
    value_c = value_f.reshape(shaped)
    gates = level_gate.reshape(NCH, STRETCH, LEVELS, HEADS)
    position = jnp.arange(STRETCH, dtype=jnp.int32)
    has_reset = offsets < STRETCH
    after_start = position[None, :] >= offsets[:, None]
    key_kept = jnp.logical_or(jnp.logical_not(has_reset)[:, None], after_start).astype(jnp.float32)
    query_open = jnp.logical_not(jnp.logical_and(has_reset[:, None], after_start)).astype(jnp.float32)
    tails = jnp.einsum('cshp,cshr->chpr', key_c * key_kept[:, :, None, None], value_c, precision=highest)
    scores = jnp.einsum('cthp,cshp->chts', query_c, key_c, precision=highest)
    causal = position[:, None] >= position[None, :]
    cut_off = has_reset[:, None, None] & after_start[:, :, None] & jnp.logical_not(after_start)[:, None, :]
    allowed = jnp.logical_and(causal[None], jnp.logical_not(cut_off)).astype(jnp.float32)
    intra_gate = jnp.transpose(gates[:, :, 0, :], (0, 2, 1))
    weights = scores * allowed[:, None] * intra_gate[:, :, :, None]
    summed = jnp.einsum('chts,cshr->cthr', weights, value_c, precision=highest)
    stretch_index = jnp.arange(NCH, dtype=jnp.int32)
    marks = jnp.where(has_reset, stretch_index, -1).astype(jnp.int32)
    before = jnp.concatenate([jnp.full((1,), -1, jnp.int32), lax.cummax(marks)[:-1]])
    blocks = tails
    flags = has_reset
    for bit_index in range(NCH.bit_length() - 1):
        owner = jnp.right_shift(stretch_index, bit_index)
        chosen = jnp.maximum(owner - 1, 0).astype(jnp.int32)
        usable = jnp.logical_and(owner % 2 == 1, before < jnp.left_shift(owner, bit_index)).astype(jnp.float32)
        state = blocks[chosen]
        product = jnp.einsum('cthp,chpr->cthr', query_c, state, precision=highest)
        scaled = gates[:, :, bit_index + 1, :] * query_open[:, :, None] * usable[:, None, None]
        summed = summed + scaled[..., None] * product
        lower = blocks[0::2]
        upper = blocks[1::2]
        blocks = jnp.where(flags[1::2][:, None, None, None], upper, lower + upper)
        flags = jnp.logical_or(flags[0::2], flags[1::2])
    return (summed.reshape(SEQLEN, HEADS * HEAD_DIM), blocks[0] * state_scale)

def one_sequence(inputs, w_full):
    queries, key_vectors, value_vectors, features, offsets, cotangent, final_grad = inputs
    feat_f = features.astype(jnp.float32)

    def forward(query_f, key_f, value_f, w_f):
        level_gate = jax.nn.softplus(jnp.dot(feat_f, w_f, precision=highest))
        mixed, final_state = sequence_forward(query_f, key_f, value_f, level_gate, offsets)
        normed = normalize(mixed.reshape(SEQLEN, HEADS, HEAD_DIM)).reshape(SEQLEN, HEADS * HEAD_DIM)
        return (normed, final_state)
    outputs, pullback = jax.vjp(forward, queries.astype(jnp.float32), key_vectors.astype(jnp.float32), value_vectors.astype(jnp.float32), w_full)
    grads = pullback((cotangent.astype(jnp.float32), final_grad.astype(jnp.float32)))
    return (outputs[0].astype(jnp.bfloat16), grads[0].astype(jnp.bfloat16), grads[1].astype(jnp.bfloat16), grads[2].astype(jnp.bfloat16), grads[3], outputs[1])

def reference(queries, key_vectors, value_vectors, features, w_level, offsets, cotangent, final_grad):
    w_full = w_level.astype(jnp.float32)
    results = lax.map(lambda inputs: one_sequence(inputs, w_full), (queries, key_vectors, value_vectors, features, offsets, cotangent, final_grad))
    return (results[0], results[1], results[2], results[3], lax.optimization_barrier(jnp.sum(results[4], 0)), results[5])
```

```python
import functools

import jax
import jax.numpy as jnp
from jax import lax
from jax.experimental import pallas as pl
from jax.experimental.pallas import tpu as pltpu
from jax.sharding import PartitionSpec as P

HEADS = 12
HEAD_DIM = 128
STRETCH = 128
LEVELS = 12
CHUNK = 2

epsilon = 1e-06
state_scale = 0.0625
f32 = jnp.float32
bf16 = jnp.bfloat16


def split(x):
    hi = x.astype(bf16)
    return hi, (x - hi.astype(f32)).astype(bf16)


def dot(a, b, dims):
    return lax.dot_general(a, b, (dims, ((), ())), preferred_element_type=f32)


NN = ((1,), (0,))
NT = ((1,), (1,))
TN = ((0,), (0,))


def bit_of(index, i):
    return lax.rem(index // (1 << i), 2)


def partner_of(index, i):
    return index + (1 << i) * (1 - 2 * bit_of(index, i))


def greet(targets):
    barrier = pltpu.get_barrier_semaphore()
    for target in targets:
        pl.semaphore_signal(barrier, inc=1, device_id=target, device_id_type=pl.DeviceIdType.MESH)
    pl.semaphore_wait(barrier, len(targets))


def remote(src, dst, send_sem, recv_sem, target):
    return pltpu.make_async_remote_copy(
        src_ref=src,
        dst_ref=dst,
        send_sem=send_sem,
        recv_sem=recv_sem,
        device_id=target,
        device_id_type=pl.DeviceIdType.MESH,
    )


def columns(h):
    return slice(h * HEAD_DIM, (h + 1) * HEAD_DIM)


def offset_plane(off_ref, j, shape):
    return jnp.full(shape, off_ref[0, j], jnp.int32)


def kept_of(off_ref, j):
    off = offset_plane(off_ref, j, (STRETCH, HEAD_DIM))
    position = lax.broadcasted_iota(jnp.int32, (STRETCH, HEAD_DIM), 0)
    return jnp.where((off >= STRETCH) | (position >= off), 1.0, 0.0).astype(f32)


def reset_of(off_ref, j):
    return jnp.where(offset_plane(off_ref, j, (8, HEAD_DIM)) < STRETCH, 1.0, 0.0).astype(f32)


def forward_kernel(bits, off_ref, k_ref, v_ref, states, tail_ref, final_ref, meta_ref, own, flags, got_flags, send, recv, fsend, frecv):
    me = lax.axis_index("seq")
    partners = [{"seq": partner_of(me, i)} for i in range(bits)]
    uppers = [bit_of(me, i) for i in range(bits)]
    greet(partners)
    heads = own.shape[1]
    chunks = heads // CHUNK
    kept = [kept_of(off_ref, j).astype(bf16) for j in range(2)]
    reset = [reset_of(off_ref, j) for j in range(2)]
    reset_up = reset[1][0:1] > 0.5
    flags[0] = jnp.maximum(reset[0], reset[1])
    prefix = [jnp.zeros((8, HEAD_DIM), f32)]

    def flag_copy(i):
        return remote(flags.at[i], got_flags.at[i], fsend.at[i], frecv.at[i], partners[i])

    def copy(i, c):
        part = pl.ds(c * CHUNK, CHUNK)
        return remote(own.at[i, part], states.at[i, part], send.at[i, c], recv.at[i, c], partners[i])

    flag_copy(0).start()
    upper_flags = []
    for wave in range(chunks + bits):
        for i in range(bits, 0, -1):
            c = wave - i
            if c < 0 or c >= chunks:
                continue
            level = i - 1
            if c == 0:
                flag_copy(level).wait_recv()
                mine, theirs = flags[level], got_flags[level]
                is_upper = jnp.full((8, HEAD_DIM), uppers[level], jnp.int32) > 0
                up = is_upper.astype(f32)
                meta_ref[level] = up * (1.0 - prefix[0])
                meta_ref[bits + level] = 1.0 - mine
                meta_ref[2 * bits + level] = 1.0 - theirs
                upper_flags.append(jnp.where(is_upper, mine, theirs))
                prefix[0] = jnp.where(is_upper, jnp.maximum(prefix[0], theirs), prefix[0])
                if i < bits:
                    flags[i] = jnp.maximum(mine, theirs)
                    flag_copy(i).start()
            copy(level, c).wait_recv()
            upper_row = jnp.full((1, HEAD_DIM), uppers[level], jnp.int32) > 0
            drop = upper_flags[level][0:1] > 0.5
            for h in range(c * CHUNK, (c + 1) * CHUNK):
                mine, theirs = own[level, h], states[level, h]
                both = jnp.where(drop, jnp.where(upper_row, mine, theirs), mine + theirs)
                if i < bits:
                    own[i, h] = both
                else:
                    final_ref[h] = both * state_scale
            if i < bits:
                copy(i, c).start()
        if wave < chunks:
            for h in range(wave * CHUNK, (wave + 1) * CHUNK):
                low = dot(k_ref[:STRETCH, columns(h)] * kept[0], v_ref[:STRETCH, columns(h)], TN)
                high = dot(k_ref[STRETCH:, columns(h)] * kept[1], v_ref[STRETCH:, columns(h)], TN)
                tail_ref[h] = low
                own[0, h] = jnp.where(reset_up, high, low + high)
            copy(0, wave).start()
    for i in range(bits):
        flag_copy(i).wait_send()
        for c in range(chunks):
            copy(i, c).wait_send()


def main_kernel(bits, off_ref, q_ref, k_ref, v_ref, g_ref, gate_ref, states, tail_ref, meta_ref,
                normed_ref, gq_ref, gk_ref, gv_ref, sg_ref, low_ref, ggate_ref):
    position = lax.broadcasted_iota(jnp.int32, (STRETCH, HEAD_DIM), 0)
    source = lax.broadcasted_iota(jnp.int32, (STRETCH, STRETCH), 1)
    gate = gate_ref[0]
    reset_low = reset_of(off_ref, 0)[0:1]
    q, k, v = q_ref[...], k_ref[...], v_ref[...]
    halves = (slice(0, STRETCH), slice(STRETCH, 2 * STRETCH))
    opens, alloweds, scores, gated, weights, intra = [], [], [], [], [], []
    for j, rows in enumerate(halves):
        off = offset_plane(off_ref, j, (STRETCH, HEAD_DIM))
        after = position >= off
        opens.append(jnp.where(after, 0.0, 1.0).astype(f32))
        allowed = jnp.where((position >= source) & jnp.logical_not(after & (source < off)), 1.0, 0.0).astype(f32)
        alloweds.append(allowed)
        scores.append(dot(q[rows], k[rows], NT))
        gated.append(allowed * gate[rows, 0:1])
        weights.append(split(scores[j] * gated[j]))
        wh, wl = weights[j]
        intra.append(dot(wh, v[rows], NN) + dot(wl, v[rows], NN))
    open_all = jnp.concatenate(opens, 0)
    near_h, near_l = split(tail_ref[0])
    near_out = dot(q[STRETCH:], near_h, NN) + dot(q[STRETCH:], near_l, NN)
    near_scale = gate[STRETCH:, 1:2] * opens[1]
    intra[1] = intra[1] + near_scale * near_out
    mixed = jnp.concatenate(intra, 0)
    ok = jnp.concatenate([jnp.ones((STRETCH, HEAD_DIM), f32), jnp.zeros((STRETCH, HEAD_DIM), f32) + (1.0 - reset_low)], 0)
    masks, products, pieces = [], [], []
    for i in range(bits):
        sh, sl = split(states[i, 0])
        pieces.append((sh, sl))
        product = dot(q, sh, NN) + dot(q, sl, NN)
        mask = open_all * ok * meta_ref[i][0:1]
        masks.append(mask)
        products.append(product)
        mixed = mixed + gate[:, 2 + i : 3 + i] * mask * product
    r = lax.rsqrt(jnp.mean(mixed * mixed, -1, keepdims=True) + epsilon)
    normed = mixed * r
    normed_ref[...] = normed.astype(bf16)
    g = g_ref[...].astype(f32)
    gs = r * (g - normed * jnp.mean(g * normed, -1, keepdims=True))
    gh, gl = split(gs)
    gq, gintra = [], []
    for j, rows in enumerate(halves):
        gw = dot(gh[rows], v[rows], NT) + dot(gl[rows], v[rows], NT)
        gintra.append(jnp.sum(gw * alloweds[j] * scores[j], -1, keepdims=True))
        sh, sl = split(gw * gated[j])
        wh, wl = weights[j]
        gv_ref[rows] = dot(wh, gh[rows], TN) + dot(wh, gl[rows], TN) + dot(wl, gh[rows], TN)
        gk_ref[rows] = dot(sh, q[rows], TN) + dot(sl, q[rows], TN)
        gq.append(dot(sh, k[rows], NN) + dot(sl, k[rows], NN))
    upper = halves[1]
    nh, nl = split(near_scale * gs[upper])
    gq[1] = gq[1] + dot(nh, near_h, NT) + dot(nh, near_l, NT) + dot(nl, near_h, NT)
    low_ref[0] = dot(q[upper], nh, TN) + dot(q[upper], nl, TN)
    gnear = jnp.sum(near_out * gs[upper] * opens[1], -1, keepdims=True)
    gates = [jnp.concatenate(gintra, 0), jnp.concatenate([jnp.zeros((STRETCH, 1), f32), gnear], 0)]
    total = jnp.concatenate(gq, 0)
    for i in range(bits):
        sh, sl = pieces[i]
        masked = masks[i] * gs
        gates.append(jnp.sum(products[i] * masked, -1, keepdims=True))
        wh, wl = split(gate[:, 2 + i : 3 + i] * masked)
        total = total + dot(wh, sh, NT) + dot(wh, sl, NT) + dot(wl, sh, NT)
        sg_ref[i, 0] = dot(q, wh, TN) + dot(q, wl, TN)
    gq_ref[...] = total.astype(bf16)
    lane = lax.broadcasted_iota(jnp.int32, (2 * STRETCH, gate.shape[1]), 1)
    out = jnp.zeros((2 * STRETCH, gate.shape[1]), f32)
    for level, column in enumerate(gates):
        out = jnp.where(lane == level, column, out)
    ggate_ref[0] = out


def backward_kernel(bits, group_bits, off_ref, k_ref, v_ref, gk_ref, gv_ref, sg_ref, low_ref, meta_ref, fin_ref, feat_ref, dl_ref,
                    gk_out, gv_out, gl_out, block, outbox, inbox, terms, got_terms, sums, got_sums,
                    send, recv, tsend, trecv, ssend, srecv):
    me = lax.axis_index("seq")
    group = lax.axis_index("dp")
    count = 1 << bits
    partners = [{"seq": partner_of(me, i)} for i in range(bits)]
    peers = [{"seq": lax.rem(me + r, count)} for r in range(1, count)]
    siblings = [{"dp": partner_of(group, i)} for i in range(group_bits)]
    greet(peers + siblings)
    heads = block.shape[0]
    chunks = heads // CHUNK

    def copy(i, c):
        part = pl.ds(c * CHUNK, CHUNK)
        return remote(outbox.at[i, part], inbox.at[i, part], send.at[i, c], recv.at[i, c], partners[i])

    def term_copy(r):
        return remote(terms.at[lax.rem(me + r, count)], got_terms.at[r - 1], tsend.at[r - 1], trecv.at[r - 1], peers[r - 1])

    def sum_copy(i):
        return remote(sums.at[i], got_sums.at[i], ssend.at[i], srecv.at[i], siblings[i])

    is_first = jnp.full((HEAD_DIM, HEAD_DIM), me, jnp.int32) == 0
    reset_up = reset_of(off_ref, 1)[0:1]
    kept = [kept_of(off_ref, j) for j in range(2)]

    def launch(i, c):
        is_upper = jnp.full((HEAD_DIM, HEAD_DIM), bit_of(me, i), jnp.int32) > 0
        own_keep = meta_ref[bits + i][0:1]
        partner_keep = meta_ref[2 * bits + i][0:1]
        for h in range(c * CHUNK, (c + 1) * CHUNK):
            current = block[h]
            outbox[i, h] = jnp.where(is_upper, current * own_keep + sg_ref[i, h], current)
            block[h] = jnp.where(is_upper, current, current * partner_keep)
        copy(i, c).start()

    def finish(c):
        for h in range(c * CHUNK, (c + 1) * CHUNK):
            current = block[h]
            first = current * (1.0 - reset_up) + low_ref[h]
            for j, state in enumerate((first, current)):
                rows = slice(j * STRETCH, (j + 1) * STRETCH)
                sh, sl = split(state)
                kk, vv = k_ref[rows, columns(h)], v_ref[rows, columns(h)]
                gk = dot(vv, sh, NT) + dot(vv, sl, NT)
                gv = dot(kk, sh, NN) + dot(kk, sl, NN)
                gk_out[rows, columns(h)] = (gk_ref[rows, columns(h)] + kept[j] * gk).astype(bf16)
                gv_out[rows, columns(h)] = (gv_ref[rows, columns(h)] + kept[j] * gv).astype(bf16)

    width = terms.shape[2]
    dh, dl = split(dl_ref[...])
    for wave in range(chunks + bits):
        for i in range(bits, 0, -1):
            c = wave - i
            if c < 0 or c >= chunks:
                continue
            level = bits - i
            copy(level, c).wait_recv()
            for h in range(c * CHUNK, (c + 1) * CHUNK):
                block[h] = block[h] + inbox[level, h]
            if level:
                launch(level - 1, c)
            else:
                finish(c)
        if wave < chunks:
            for h in range(wave * CHUNK, (wave + 1) * CHUNK):
                block[h] = jnp.where(is_first, fin_ref[h].astype(f32) * state_scale, 0.0)
            launch(bits - 1, wave)
        if wave == 0:
            for n in range(count):
                part = feat_ref[:, n * width : (n + 1) * width]
                terms[n] = dot(dh, part, NN) + dot(dl, part, NN)
            for r in range(1, count):
                term_copy(r).start()
        if wave == chunks:
            total = terms[me]
            for r in range(1, count):
                term_copy(r).wait_recv()
                total = total + got_terms[r - 1]
            if group_bits:
                sums[0] = total
                sum_copy(0).start()
            else:
                gl_out[...] = total
    for i in range(group_bits):
        sum_copy(i).wait_recv()
        total = sums[i] + got_sums[i]
        if i + 1 < group_bits:
            sums[i + 1] = total
            sum_copy(i + 1).start()
        else:
            gl_out[...] = total
    for i in range(bits):
        for c in range(chunks):
            copy(i, c).wait_send()
    for r in range(1, count):
        term_copy(r).wait_send()
    for i in range(group_bits):
        sum_copy(i).wait_send()


def body(queries, key_vectors, value_vectors, features, w_level, offsets, cotangent, final_grad):
    count = lax.axis_size("seq")
    groups = lax.axis_size("dp")
    bits = count.bit_length() - 1
    group_bits = groups.bit_length() - 1
    used = bits + 2
    model = features.shape[-1]
    heads = queries.shape[-1] // HEAD_DIM
    length = queries.shape[1]
    q, k, v, g, feat = queries[0], key_vectors[0], value_vectors[0], cotangent[0], features[0]
    vmem = pl.BlockSpec(memory_space=pltpu.VMEM)
    smem = pl.BlockSpec(memory_space=pltpu.SMEM)
    state = (heads, HEAD_DIM, HEAD_DIM)
    chunks = heads // CHUNK
    sds = jax.ShapeDtypeStruct
    sem = pltpu.SemaphoreType.DMA
    big = pltpu.CompilerParams(vmem_limit_bytes=60 * 1024 * 1024)

    states, tails, final_state, meta = pl.pallas_call(
        functools.partial(forward_kernel, bits),
        out_shape=(sds((bits,) + state, f32), sds(state, f32), sds(state, f32), sds((3 * bits, 8, HEAD_DIM), f32)),
        in_specs=[smem, vmem, vmem],
        out_specs=(vmem,) * 4,
        scratch_shapes=[
            pltpu.VMEM((bits,) + state, f32),
            pltpu.VMEM((bits, 8, HEAD_DIM), f32),
            pltpu.VMEM((bits, 8, HEAD_DIM), f32),
            sem((bits, chunks)), sem((bits, chunks)), sem((bits,)), sem((bits,)),
        ],
        compiler_params=pltpu.CompilerParams(collective_id=0, has_side_effects=True, vmem_limit_bytes=60 * 1024 * 1024),
        name="forward_exchange",
    )(offsets, k, v)

    w_used = jnp.transpose(w_level.reshape(model, LEVELS, heads)[:, :used], (0, 2, 1))
    logit = jnp.einsum("td,dhl->htl", feat, w_used, preferred_element_type=f32)
    gate = jax.nn.softplus(logit)

    head = pl.BlockSpec((length, HEAD_DIM), lambda h: (0, h))
    gates = pl.BlockSpec((1, length, used), lambda h: (h, 0, 0))
    one = pl.BlockSpec((1, HEAD_DIM, HEAD_DIM), lambda h: (h, 0, 0))
    many = pl.BlockSpec((bits, 1, HEAD_DIM, HEAD_DIM), lambda h: (0, h, 0, 0))
    flat = sds((length, heads * HEAD_DIM), bf16)
    flat_f = sds((length, heads * HEAD_DIM), f32)
    normed, gq, gk, gv, sg, low, ggate = pl.pallas_call(
        functools.partial(main_kernel, bits),
        grid=(heads,),
        out_shape=(flat, flat, flat_f, flat_f, sds((bits,) + state, f32), sds(state, f32), sds((heads, length, used), f32)),
        in_specs=[smem, head, head, head, head, gates, many, one, pl.BlockSpec((3 * bits, 8, HEAD_DIM), lambda h: (0, 0, 0))],
        out_specs=(head, head, head, head, many, one, gates),
        compiler_params=big,
        name="local_passes",
    )(offsets, q, k, v, g, gate, states, tails, meta)

    dlogit = ggate * jax.nn.sigmoid(logit)
    rows = -(-used * heads // 8) * 8
    dl = jnp.transpose(dlogit, (2, 0, 1)).reshape(used * heads, length)
    dl = jnp.pad(dl, ((0, rows - used * heads), (0, 0)))
    width = model // count
    slab = (rows, width)
    gk, gv, gl = pl.pallas_call(
        functools.partial(backward_kernel, bits, group_bits),
        out_shape=(flat, flat, sds(slab, f32)),
        in_specs=[smem] + [vmem] * 10,
        out_specs=(vmem,) * 3,
        scratch_shapes=[
            pltpu.VMEM(state, f32),
            pltpu.VMEM((bits,) + state, f32),
            pltpu.VMEM((bits,) + state, f32),
            pltpu.VMEM((count,) + slab, f32),
            pltpu.VMEM((count - 1,) + slab, f32),
            pltpu.VMEM((max(group_bits, 1),) + slab, f32),
            pltpu.VMEM((max(group_bits, 1),) + slab, f32),
            sem((bits, chunks)), sem((bits, chunks)), sem((count - 1,)), sem((count - 1,)),
            sem((max(group_bits, 1),)), sem((max(group_bits, 1),)),
        ],
        compiler_params=pltpu.CompilerParams(collective_id=1, has_side_effects=True, vmem_limit_bytes=60 * 1024 * 1024),
        name="backward_exchange",
    )(offsets, k, v, gk, gv, sg, low, meta, final_grad[0], feat, dl)
    grad_level = jnp.pad(gl[: used * heads].T, ((0, 0), (0, (LEVELS - used) * heads)))
    return normed[None], gq[None], gk[None], gv[None], grad_level, final_state[None]


def solution(mesh):
    in_specs = (
        P("dp", "seq", None),
        P("dp", "seq", None),
        P("dp", "seq", None),
        P("dp", "seq", None),
        P(),
        P("dp", "seq"),
        P("dp", "seq", None),
        P("dp", None, None, None),
    )
    out_specs = (
        P("dp", "seq", None),
        P("dp", "seq", None),
        P("dp", "seq", None),
        P("dp", "seq", None),
        P("seq", None),
        P("dp", None, None, None),
    )
    return jax.shard_map(body, mesh=mesh, in_specs=in_specs, out_specs=out_specs, check_vma=False)
```

```python
import functools

import jax
import jax.numpy as jnp
from jax import lax
from jax.experimental import pallas as pl
from jax.experimental.pallas import tpu as pltpu
from jax.sharding import PartitionSpec as P

HEADS = 12
HEAD_DIM = 128
STRETCH = 128
LEVELS = 12

epsilon = 1e-06
state_scale = 0.0625
f32 = jnp.float32
bf16 = jnp.bfloat16


def split(x):
    hi = x.astype(bf16)
    return hi, (x - hi.astype(f32)).astype(bf16)


def dot(a, b, dims):
    return lax.dot_general(a, b, (dims, ((), ())), preferred_element_type=f32)


NN = ((1,), (0,))
NT = ((1,), (1,))
TN = ((0,), (0,))


def bit_of(index, i):
    return lax.rem(index // (1 << i), 2)


def partner_of(index, i):
    return index + (1 << i) * (1 - 2 * bit_of(index, i))


def greet(targets):
    barrier = pltpu.get_barrier_semaphore()
    for target in targets:
        pl.semaphore_signal(barrier, inc=1, device_id=target, device_id_type=pl.DeviceIdType.MESH)
    pl.semaphore_wait(barrier, len(targets))


def remote(src, dst, send_sem, recv_sem, target):
    return pltpu.make_async_remote_copy(
        src_ref=src,
        dst_ref=dst,
        send_sem=send_sem,
        recv_sem=recv_sem,
        device_id=target,
        device_id_type=pl.DeviceIdType.MESH,
    )


def columns(h):
    return slice(h * HEAD_DIM, (h + 1) * HEAD_DIM)


def offset_plane(off_ref, j, shape):
    return jnp.full(shape, off_ref[0, j], jnp.int32)


def kept_of(off_ref, j):
    off = offset_plane(off_ref, j, (STRETCH, HEAD_DIM))
    position = lax.broadcasted_iota(jnp.int32, (STRETCH, HEAD_DIM), 0)
    return jnp.where((off >= STRETCH) | (position >= off), 1.0, 0.0).astype(f32)


def reset_of(off_ref, j):
    return jnp.where(offset_plane(off_ref, j, (8, HEAD_DIM)) < STRETCH, 1.0, 0.0).astype(f32)


def fused_kernel(bits, group_bits, used, off_ref, q_ref, k_ref, v_ref, g_ref, feat_ref, w_ref, fin_ref,
                 normed_ref, gq_ref, gk_ref, gv_ref, final_ref, gl_out,
                 own, states, tails, own_flag, all_flags, meta, logits, slopes, gate_grads, gk_part, gv_part,
                 sg, low, block, outbox, inbox, terms, got_terms, sums, got_sums,
                 fsend, frecv, send, recv, bsend, brecv, tsend, trecv, ssend, srecv):
    me = lax.axis_index("seq")
    group = lax.axis_index("dp")
    count = 1 << bits
    heads = block.shape[0]
    partners = [{"seq": partner_of(me, i)} for i in range(bits)]
    uppers = [bit_of(me, i) for i in range(bits)]
    peers = [{"seq": lax.rem(me + r, count)} for r in range(1, count)]
    siblings = [{"dp": partner_of(group, i)} for i in range(group_bits)]
    square = (HEAD_DIM, HEAD_DIM)
    greet(peers + siblings)

    def lanes(h):
        return pl.ds(pl.multiple_of(h * HEAD_DIM, HEAD_DIM), HEAD_DIM)

    def flag_copy(r, owner):
        return remote(own_flag, all_flags.at[owner], fsend.at[r - 1], frecv.at[r - 1], peers[r - 1])

    def copy(i, h):
        return remote(own.at[i, h], states.at[i, h], send.at[i, h], recv.at[i, h], partners[i])

    def back_copy(i, h):
        return remote(outbox.at[i, h], inbox.at[i, h], bsend.at[i, h], brecv.at[i, h], partners[i])

    def term_copy(r):
        return remote(terms.at[lax.rem(me + r, count)], got_terms.at[r - 1], tsend.at[r - 1], trecv.at[r - 1], peers[r - 1])

    def sum_copy(i):
        return remote(sums.at[i], got_sums.at[i], ssend.at[i], srecv.at[i], siblings[i])

    def above(i, shape):
        return jnp.full(shape, uppers[i], jnp.int32) > 0

    own_flag[...] = jnp.maximum(reset_of(off_ref, 0), reset_of(off_ref, 1))
    all_flags[me] = own_flag[...]
    for r in range(1, count):
        flag_copy(r, me).start()

    def set_meta():
        for r in range(1, count):
            flag_copy(r, lax.rem(me - r + count, count)).wait_recv()
        prefix = jnp.zeros((8, HEAD_DIM), f32)
        for i in range(bits):
            base = (me // (1 << i)) * (1 << i)
            other = base + (1 << i) * (1 - 2 * uppers[i])
            mine, theirs = all_flags[base], all_flags[other]
            for j in range(1, 1 << i):
                mine = jnp.maximum(mine, all_flags[base + j])
                theirs = jnp.maximum(theirs, all_flags[other + j])
            is_upper = above(i, (8, HEAD_DIM))
            meta[i] = is_upper.astype(f32) * (1.0 - prefix)
            meta[bits + i] = 1.0 - mine
            meta[2 * bits + i] = 1.0 - theirs
            meta[3 * bits + i] = jnp.where(is_upper, mine, theirs)
            prefix = jnp.where(is_upper, jnp.maximum(prefix, theirs), prefix)

    def make_tail(h):
        kk, vv = k_ref[:, lanes(h)], v_ref[:, lanes(h)]
        tail = []
        for j in range(2):
            rows = slice(j * STRETCH, (j + 1) * STRETCH)
            tail.append(dot(kk[rows] * kept_of(off_ref, j).astype(bf16), vv[rows], TN))
        tails[h] = tail[0]
        own[0, h] = jnp.where(reset_of(off_ref, 1)[0:1] > 0.5, tail[1], tail[0] + tail[1])
        copy(0, h).start()

    def combine(i, h):
        copy(i, h).wait_recv()
        mine, theirs = own[i, h], states[i, h]
        drop = meta[3 * bits + i][0:1] > 0.5
        both = jnp.where(drop, jnp.where(above(i, square), mine, theirs), mine + theirs)
        if i + 1 < bits:
            own[i + 1, h] = both
            copy(i + 1, h).start()
        else:
            final_ref[h] = both * state_scale

    def local_passes(h):
        position = lax.broadcasted_iota(jnp.int32, (STRETCH, HEAD_DIM), 0)
        source = lax.broadcasted_iota(jnp.int32, (STRETCH, STRETCH), 1)
        table = logits[...]
        table_lane = lax.broadcasted_iota(jnp.int32, table.shape, 1)

        def gate_of(level):
            x = jnp.sum(jnp.where(table_lane == level * heads + h, table, 0.0), -1, keepdims=True)
            return x

        gate = [gate_of(level) for level in range(used)]
        reset_low = reset_of(off_ref, 0)[0:1]
        q, k, v = q_ref[:, lanes(h)], k_ref[:, lanes(h)], v_ref[:, lanes(h)]
        halves = (slice(0, STRETCH), slice(STRETCH, 2 * STRETCH))
        opens, alloweds, scores, gated, weights, intra = [], [], [], [], [], []
        for j, rows in enumerate(halves):
            off = offset_plane(off_ref, j, (STRETCH, HEAD_DIM))
            after = position >= off
            opens.append(jnp.where(after, 0.0, 1.0).astype(f32))
            allowed = jnp.where((position >= source) & jnp.logical_not(after & (source < off)), 1.0, 0.0).astype(f32)
            alloweds.append(allowed)
            scores.append(dot(q[rows], k[rows], NT))
            gated.append(allowed * gate[0][rows])
            weights.append(split(scores[j] * gated[j]))
            wh, wl = weights[j]
            intra.append(dot(wh, v[rows], NN) + dot(wl, v[rows], NN))
        open_all = jnp.concatenate(opens, 0)
        near_h, near_l = split(tails[h])
        near_out = dot(q[STRETCH:], near_h, NN) + dot(q[STRETCH:], near_l, NN)
        near_scale = gate[1][STRETCH:] * opens[1]
        intra[1] = intra[1] + near_scale * near_out
        mixed = jnp.concatenate(intra, 0)
        ok = jnp.concatenate([jnp.ones((STRETCH, HEAD_DIM), f32), jnp.zeros((STRETCH, HEAD_DIM), f32) + (1.0 - reset_low)], 0)
        masks, products, pieces = [], [], []
        for i in range(bits):
            sh, sl = split(states[i, h])
            pieces.append((sh, sl))
            product = dot(q, sh, NN) + dot(q, sl, NN)
            mask = open_all * ok * meta[i][0:1]
            masks.append(mask)
            products.append(product)
            mixed = mixed + gate[2 + i] * mask * product
        r = lax.rsqrt(jnp.mean(mixed * mixed, -1, keepdims=True) + epsilon)
        normed = mixed * r
        normed_ref[:, lanes(h)] = normed.astype(bf16)
        g = g_ref[:, lanes(h)].astype(f32)
        gs = r * (g - normed * jnp.mean(g * normed, -1, keepdims=True))
        gh, gl = split(gs)
        gq, gintra = [], []
        for j, rows in enumerate(halves):
            gw = dot(gh[rows], v[rows], NT) + dot(gl[rows], v[rows], NT)
            gintra.append(jnp.sum(gw * alloweds[j] * scores[j], -1, keepdims=True))
            sh, sl = split(gw * gated[j])
            wh, wl = weights[j]
            gv_part[h, rows] = dot(wh, gh[rows], TN) + dot(wh, gl[rows], TN) + dot(wl, gh[rows], TN)
            gk_part[h, rows] = dot(sh, q[rows], TN) + dot(sl, q[rows], TN)
            gq.append(dot(sh, k[rows], NN) + dot(sl, k[rows], NN))
        upper = halves[1]
        nh, nl = split(near_scale * gs[upper])
        gq[1] = gq[1] + dot(nh, near_h, NT) + dot(nh, near_l, NT) + dot(nl, near_h, NT)
        low[h] = dot(q[upper], nh, TN) + dot(q[upper], nl, TN)
        gnear = jnp.sum(near_out * gs[upper] * opens[1], -1, keepdims=True)
        gates = [jnp.concatenate(gintra, 0), jnp.concatenate([jnp.zeros((STRETCH, 1), f32), gnear], 0)]
        total = jnp.concatenate(gq, 0)
        for i in reversed(range(bits)):
            sh, sl = pieces[i]
            masked = masks[i] * gs
            gates.insert(2, jnp.sum(products[i] * masked, -1, keepdims=True))
            wh, wl = split(gate[2 + i] * masked)
            state_grad = dot(q, wh, TN) + dot(q, wl, TN)
            if i + 1 == bits:
                outbox[i, h] = state_grad
                grad = fin_ref[h].astype(f32) * state_scale
                first = jnp.full(square, lax.rem(me, count // 2), jnp.int32) == 0
                keep = jnp.where(above(i, square), 1.0, meta[2 * bits + i][0:1])
                block[h] = jnp.where(first, grad, 0.0) * keep

                @pl.when(uppers[i] == 1)
                def _():
                    back_copy(i, h).start()
            else:
                sg[i, h] = state_grad
            total = total + dot(wh, sh, NT) + dot(wh, sl, NT) + dot(wl, sh, NT)
        gq_ref[:, lanes(h)] = total.astype(bf16)
        out = gate_grads[...]
        for level, column in enumerate(gates):
            out = jnp.where(table_lane == level * heads + h, column, out)
        gate_grads[...] = out

    def collect(i, h):
        top = i + 1 == bits
        if top:
            @pl.when(uppers[i] == 0)
            def _():
                back_copy(i, h).wait_recv()
                block[h] = block[h] + inbox[i, h]
        else:
            back_copy(i, h).wait_recv()
            block[h] = block[h] + inbox[i, h]
        if i:
            low_level = i - 1
            current = block[h]
            is_upper = above(low_level, square)
            own_keep = meta[bits + low_level][0:1]
            partner_keep = meta[2 * bits + low_level][0:1]
            outbox[low_level, h] = jnp.where(is_upper, current * own_keep + sg[low_level, h], current)
            block[h] = jnp.where(is_upper, current, current * partner_keep)
            back_copy(low_level, h).start()
        else:
            finish(h)

    def finish(h):
        current = block[h]
        first = current * (1.0 - reset_of(off_ref, 1)[0:1]) + low[h]
        kk, vv = k_ref[:, lanes(h)], v_ref[:, lanes(h)]
        for j, state in enumerate((first, current)):
            rows = slice(j * STRETCH, (j + 1) * STRETCH)
            sh, sl = split(state)
            kept = kept_of(off_ref, j)
            gk = dot(vv[rows], sh, NT) + dot(vv[rows], sl, NT)
            gv = dot(kk[rows], sh, NN) + dot(kk[rows], sl, NN)
            gk_ref[rows, lanes(h)] = (gk_part[h, rows] + kept * gk).astype(bf16)
            gv_ref[rows, lanes(h)] = (gv_part[h, rows] + kept * gv).astype(bf16)

    def prepare_gates():
        x = dot(feat_ref[...], w_ref[...], NN)
        logits[...] = jnp.maximum(x, 0.0) + jnp.log1p(jnp.exp(-jnp.abs(x)))
        gate_grads[...] = jnp.zeros(gate_grads.shape, f32)
        slopes[...] = 1.0 / (1.0 + jnp.exp(-x))

    def reduce_gates():
        rows, width = terms.shape[1:]
        dh, dl = split((gate_grads[...] * slopes[...])[:, :rows])
        for n in range(count):
            part = feat_ref[:, n * width : (n + 1) * width]
            terms[n] = dot(dh, part, TN) + dot(dl, part, TN)
        for r in range(1, count):
            term_copy(r).start()

    stages = [make_tail]
    for i in range(bits):
        stages.append(functools.partial(combine, i))
    stages[-1] = lambda h: (combine(bits - 1, h), local_passes(h))
    for i in reversed(range(bits)):
        stages.append(functools.partial(collect, i))
    lag = 2
    passes_at = lag * bits

    def step(wave, carry):
        for depth, stage in enumerate(stages):
            h = wave - depth * lag

            @pl.when((h >= 0) & (h < heads))
            def _():
                stage(h)

            if depth == 0:
                @pl.when(wave == 1)
                def _():
                    set_meta()
                    prepare_gates()
            if depth == bits:
                @pl.when(wave == passes_at + heads - 1)
                def _():
                    reduce_gates()
        return carry

    lax.fori_loop(0, heads + lag * (len(stages) - 1), step, 0)
    total = terms[me]
    for r in range(1, count):
        term_copy(r).wait_recv()
        total = total + got_terms[r - 1]
    for i in range(group_bits):
        sums[i] = total
        sum_copy(i).start()
        sum_copy(i).wait_recv()
        total = sums[i] + got_sums[i]
    gl_out[...] = total

    def drain(h, carry):
        for i in range(bits):
            copy(i, h).wait_send()
            if i + 1 < bits:
                back_copy(i, h).wait_send()
            else:
                @pl.when(uppers[i] == 1)
                def _():
                    back_copy(i, h).wait_send()
        return carry

    lax.fori_loop(0, heads, drain, 0)
    for r in range(1, count):
        flag_copy(r, me).wait_send()
        term_copy(r).wait_send()
    for i in range(group_bits):
        sum_copy(i).wait_send()


def body(queries, key_vectors, value_vectors, features, w_level, offsets, cotangent, final_grad):
    count = lax.axis_size("seq")
    groups = lax.axis_size("dp")
    bits = count.bit_length() - 1
    group_bits = groups.bit_length() - 1
    used = bits + 2
    model = features.shape[-1]
    heads = queries.shape[-1] // HEAD_DIM
    length = queries.shape[1]
    q, k, v, g, feat = queries[0], key_vectors[0], value_vectors[0], cotangent[0], features[0]
    vmem = pl.BlockSpec(memory_space=pltpu.VMEM)
    smem = pl.BlockSpec(memory_space=pltpu.SMEM)
    state = (heads, HEAD_DIM, HEAD_DIM)
    sds = jax.ShapeDtypeStruct
    sem = pltpu.SemaphoreType.DMA
    flat = sds((length, heads * HEAD_DIM), bf16)
    rows = -(-used * heads // 8) * 8
    slab = (rows, model // count)
    table = pltpu.VMEM((length, w_level.shape[1]), f32)
    many = pltpu.VMEM((bits,) + state, f32)
    single = pltpu.VMEM(state, f32)
    part = pltpu.VMEM((heads, length, HEAD_DIM), f32)
    steps = max(group_bits, 1)
    normed, gq, gk, gv, final_state, gl = pl.pallas_call(
        functools.partial(fused_kernel, bits, group_bits, used),
        out_shape=(flat, flat, flat, flat, sds(state, f32), sds(slab, f32)),
        in_specs=[smem] + [vmem] * 7,
        out_specs=(vmem,) * 6,
        scratch_shapes=[
            many, many, single,
            pltpu.VMEM((8, HEAD_DIM), f32),
            pltpu.VMEM((count, 8, HEAD_DIM), f32),
            pltpu.VMEM((4 * bits, 8, HEAD_DIM), f32),
            table, table, table, part, part,
            many, single, single, many, many,
            pltpu.VMEM((count,) + slab, f32),
            pltpu.VMEM((count - 1,) + slab, f32),
            pltpu.VMEM((steps,) + slab, f32),
            pltpu.VMEM((steps,) + slab, f32),
            sem((count - 1,)), sem((count - 1,)),
            sem((bits, heads)), sem((bits, heads)), sem((bits, heads)), sem((bits, heads)),
            sem((count - 1,)), sem((count - 1,)), sem((steps,)), sem((steps,)),
        ],
        compiler_params=pltpu.CompilerParams(collective_id=0, has_side_effects=True, vmem_limit_bytes=62 * 1024 * 1024),
        name="fused_layer",
    )(offsets, q, k, v, g, feat, w_level, final_grad[0])
    grad_level = jnp.pad(gl[: used * heads].T, ((0, 0), (0, (LEVELS - used) * heads)))
    return normed[None], gq[None], gk[None], gv[None], grad_level, final_state[None]


def solution(mesh):
    in_specs = (
        P("dp", "seq", None),
        P("dp", "seq", None),
        P("dp", "seq", None),
        P("dp", "seq", None),
        P(),
        P("dp", "seq"),
        P("dp", "seq", None),
        P("dp", None, None, None),
    )
    out_specs = (
        P("dp", "seq", None),
        P("dp", "seq", None),
        P("dp", "seq", None),
        P("dp", "seq", None),
        P("seq", None),
        P("dp", None, None, None),
    )
    return jax.shard_map(body, mesh=mesh, in_specs=in_specs, out_specs=out_specs, check_vma=False)
```

```python
import functools

import jax
import jax.numpy as jnp
from jax import lax
from jax.experimental import pallas as pl
from jax.experimental.pallas import tpu as pltpu
from jax.sharding import PartitionSpec as P

HEADS = 12
HEAD_DIM = 128
STRETCH = 128
LEVELS = 12

epsilon = 1e-06
state_scale = 0.0625
f32 = jnp.float32
bf16 = jnp.bfloat16


def split(x):
    hi = x.astype(bf16)
    return hi, (x - hi.astype(f32)).astype(bf16)


def dot(a, b, dims):
    return lax.dot_general(a, b, (dims, ((), ())), preferred_element_type=f32)


NN = ((1,), (0,))
NT = ((1,), (1,))
TN = ((0,), (0,))


def bit_of(index, i):
    return lax.rem(index // (1 << i), 2)


def partner_of(index, i):
    return index + (1 << i) * (1 - 2 * bit_of(index, i))


def greet(targets):
    barrier = pltpu.get_barrier_semaphore()
    for target in targets:
        pl.semaphore_signal(barrier, inc=1, device_id=target, device_id_type=pl.DeviceIdType.MESH)
    pl.semaphore_wait(barrier, len(targets))


def remote(src, dst, send_sem, recv_sem, target):
    return pltpu.make_async_remote_copy(
        src_ref=src,
        dst_ref=dst,
        send_sem=send_sem,
        recv_sem=recv_sem,
        device_id=target,
        device_id_type=pl.DeviceIdType.MESH,
    )


def columns(h):
    return slice(h * HEAD_DIM, (h + 1) * HEAD_DIM)


def offset_plane(off_ref, j, shape):
    return jnp.full(shape, off_ref[0, j], jnp.int32)


def kept_of(off_ref, j):
    off = offset_plane(off_ref, j, (STRETCH, HEAD_DIM))
    position = lax.broadcasted_iota(jnp.int32, (STRETCH, HEAD_DIM), 0)
    return jnp.where((off >= STRETCH) | (position >= off), 1.0, 0.0).astype(f32)


def reset_of(off_ref, j):
    return jnp.where(offset_plane(off_ref, j, (8, HEAD_DIM)) < STRETCH, 1.0, 0.0).astype(f32)


def fused_kernel(bits, group_bits, used, off_ref, q_ref, k_ref, v_ref, g_ref, feat_ref, w_ref, fin_ref,
                 normed_ref, gq_ref, gk_ref, gv_ref, final_ref, gl_out,
                 own, states, tails, own_flag, all_flags, meta, logits, slopes, gate_grads, gk_part, gv_part,
                 sg, low, block, outbox, inbox, terms, got_terms, sums, got_sums,
                 fsend, frecv, send, recv, bsend, brecv, tsend, trecv, ssend, srecv, hsend, hrecv):
    me = lax.axis_index("seq")
    group = lax.axis_index("dp")
    count = 1 << bits
    heads = block.shape[0]
    partners = [{"seq": partner_of(me, i)} for i in range(bits)]
    uppers = [bit_of(me, i) for i in range(bits)]
    peers = [{"seq": lax.rem(me + r, count)} for r in range(1, count)]
    siblings = [{"dp": partner_of(group, i)} for i in range(group_bits)]
    square = (HEAD_DIM, HEAD_DIM)
    greet(peers + siblings)

    def lanes(h):
        return pl.ds(pl.multiple_of(h * HEAD_DIM, HEAD_DIM), HEAD_DIM)

    def flag_copy(r, owner):
        return remote(own_flag, all_flags.at[owner], fsend.at[r - 1], frecv.at[r - 1], peers[r - 1])

    def copy(i, h):
        return remote(own.at[i, h], states.at[i, h], send.at[i, h], recv.at[i, h], partners[i])

    def back_copy(i, h):
        return remote(outbox.at[i, h], inbox.at[i, h], bsend.at[i, h], brecv.at[i, h], partners[i])

    def term_copy(r):
        return remote(terms.at[lax.rem(me + r, count)], got_terms.at[r - 1], tsend.at[r - 1], trecv.at[r - 1], peers[r - 1])

    def sum_copy(i):
        return remote(sums.at[i], got_sums.at[i], ssend.at[i], srecv.at[i], siblings[i])

    half = count // 2
    place = lax.rem(me, half)
    is_low = uppers[bits - 1] == 0
    mates = [{"seq": me - place + lax.rem(place + r, half)} for r in range(1, half)]

    def leads(h):
        return lax.rem(h, half) == place

    def shares(h):
        return is_low & leads(h)

    def sends_top(h):
        return is_low | leads(h)

    def share_copy(h, r):
        return remote(final_ref.at[h], final_ref.at[h], hsend.at[h, r - 1], hrecv.at[h], mates[r - 1])

    def above(i, shape):
        return jnp.full(shape, uppers[i], jnp.int32) > 0

    own_flag[...] = jnp.maximum(reset_of(off_ref, 0), reset_of(off_ref, 1))
    all_flags[me] = own_flag[...]
    for r in range(1, count):
        flag_copy(r, me).start()

    def set_meta():
        for r in range(1, count):
            flag_copy(r, lax.rem(me - r + count, count)).wait_recv()
        prefix = jnp.zeros((8, HEAD_DIM), f32)
        for i in range(bits):
            base = (me // (1 << i)) * (1 << i)
            other = base + (1 << i) * (1 - 2 * uppers[i])
            mine, theirs = all_flags[base], all_flags[other]
            for j in range(1, 1 << i):
                mine = jnp.maximum(mine, all_flags[base + j])
                theirs = jnp.maximum(theirs, all_flags[other + j])
            is_upper = above(i, (8, HEAD_DIM))
            meta[i] = is_upper.astype(f32) * (1.0 - prefix)
            meta[bits + i] = 1.0 - mine
            meta[2 * bits + i] = 1.0 - theirs
            meta[3 * bits + i] = jnp.where(is_upper, mine, theirs)
            prefix = jnp.where(is_upper, jnp.maximum(prefix, theirs), prefix)

    def make_tail(h):
        kk, vv = k_ref[:, lanes(h)], v_ref[:, lanes(h)]
        tail = []
        for j in range(2):
            rows = slice(j * STRETCH, (j + 1) * STRETCH)
            tail.append(dot(kk[rows] * kept_of(off_ref, j).astype(bf16), vv[rows], TN))
        tails[h] = tail[0]
        own[0, h] = jnp.where(reset_of(off_ref, 1)[0:1] > 0.5, tail[1], tail[0] + tail[1])
        copy(0, h).start()

    def combine(i, h):
        def joined():
            mine, theirs = own[i, h], states[i, h]
            drop = meta[3 * bits + i][0:1] > 0.5
            return jnp.where(drop, jnp.where(above(i, square), mine, theirs), mine + theirs)

        if i + 1 < bits:
            copy(i, h).wait_recv()
            own[i + 1, h] = joined()
            if i + 2 < bits:
                copy(i + 1, h).start()
            else:
                @pl.when(sends_top(h))
                def _():
                    copy(i + 1, h).start()
        else:
            @pl.when((uppers[i] == 1) | leads(h))
            def _():
                copy(i, h).wait_recv()
                final_ref[h] = joined() * state_scale

            @pl.when(shares(h))
            def _():
                for r in range(1, half):
                    share_copy(h, r).start()

    def local_passes(h):
        position = lax.broadcasted_iota(jnp.int32, (STRETCH, HEAD_DIM), 0)
        source = lax.broadcasted_iota(jnp.int32, (STRETCH, STRETCH), 1)
        table = logits[...]
        table_lane = lax.broadcasted_iota(jnp.int32, table.shape, 1)

        def gate_of(level):
            x = jnp.sum(jnp.where(table_lane == level * heads + h, table, 0.0), -1, keepdims=True)
            return x

        gate = [gate_of(level) for level in range(used)]
        reset_low = reset_of(off_ref, 0)[0:1]
        q, k, v = q_ref[:, lanes(h)], k_ref[:, lanes(h)], v_ref[:, lanes(h)]
        halves = (slice(0, STRETCH), slice(STRETCH, 2 * STRETCH))
        opens, alloweds, scores, gated, weights, intra = [], [], [], [], [], []
        for j, rows in enumerate(halves):
            off = offset_plane(off_ref, j, (STRETCH, HEAD_DIM))
            after = position >= off
            opens.append(jnp.where(after, 0.0, 1.0).astype(f32))
            allowed = jnp.where((position >= source) & jnp.logical_not(after & (source < off)), 1.0, 0.0).astype(f32)
            alloweds.append(allowed)
            scores.append(dot(q[rows], k[rows], NT))
            gated.append(allowed * gate[0][rows])
            weights.append(split(scores[j] * gated[j]))
            wh, wl = weights[j]
            intra.append(dot(wh, v[rows], NN) + dot(wl, v[rows], NN))
        open_all = jnp.concatenate(opens, 0)
        near_h, near_l = split(tails[h])
        near_out = dot(q[STRETCH:], near_h, NN) + dot(q[STRETCH:], near_l, NN)
        near_scale = gate[1][STRETCH:] * opens[1]
        intra[1] = intra[1] + near_scale * near_out
        mixed = jnp.concatenate(intra, 0)
        ok = jnp.concatenate([jnp.ones((STRETCH, HEAD_DIM), f32), jnp.zeros((STRETCH, HEAD_DIM), f32) + (1.0 - reset_low)], 0)
        masks, products, pieces = [], [], []
        for i in range(bits):
            sh, sl = split(states[i, h])
            pieces.append((sh, sl))
            product = dot(q, sh, NN) + dot(q, sl, NN)
            mask = open_all * ok * meta[i][0:1]
            masks.append(mask)
            products.append(product)
            mixed = mixed + gate[2 + i] * mask * product
        r = lax.rsqrt(jnp.mean(mixed * mixed, -1, keepdims=True) + epsilon)
        normed = mixed * r
        normed_ref[:, lanes(h)] = normed.astype(bf16)
        g = g_ref[:, lanes(h)].astype(f32)
        gs = r * (g - normed * jnp.mean(g * normed, -1, keepdims=True))
        gh, gl = split(gs)
        gq, gintra = [], []
        for j, rows in enumerate(halves):
            gw = dot(gh[rows], v[rows], NT) + dot(gl[rows], v[rows], NT)
            gintra.append(jnp.sum(gw * alloweds[j] * scores[j], -1, keepdims=True))
            sh, sl = split(gw * gated[j])
            wh, wl = weights[j]
            gv_part[h, rows] = dot(wh, gh[rows], TN) + dot(wh, gl[rows], TN) + dot(wl, gh[rows], TN)
            gk_part[h, rows] = dot(sh, q[rows], TN) + dot(sl, q[rows], TN)
            gq.append(dot(sh, k[rows], NN) + dot(sl, k[rows], NN))
        upper = halves[1]
        nh, nl = split(near_scale * gs[upper])
        gq[1] = gq[1] + dot(nh, near_h, NT) + dot(nh, near_l, NT) + dot(nl, near_h, NT)
        low[h] = dot(q[upper], nh, TN) + dot(q[upper], nl, TN)
        gnear = jnp.sum(near_out * gs[upper] * opens[1], -1, keepdims=True)
        gates = [jnp.concatenate(gintra, 0), jnp.concatenate([jnp.zeros((STRETCH, 1), f32), gnear], 0)]
        total = jnp.concatenate(gq, 0)
        for i in reversed(range(bits)):
            sh, sl = pieces[i]
            masked = masks[i] * gs
            gates.insert(2, jnp.sum(products[i] * masked, -1, keepdims=True))
            wh, wl = split(gate[2 + i] * masked)
            state_grad = dot(q, wh, TN) + dot(q, wl, TN)
            if i + 1 == bits:
                outbox[i, h] = state_grad
                grad = fin_ref[h].astype(f32) * state_scale
                first = jnp.full(square, lax.rem(me, count // 2), jnp.int32) == 0
                keep = jnp.where(above(i, square), 1.0, meta[2 * bits + i][0:1])
                block[h] = jnp.where(first, grad, 0.0) * keep

                @pl.when(uppers[i] == 1)
                def _():
                    back_copy(i, h).start()
            else:
                sg[i, h] = state_grad
            total = total + dot(wh, sh, NT) + dot(wh, sl, NT) + dot(wl, sh, NT)
        gq_ref[:, lanes(h)] = total.astype(bf16)
        out = gate_grads[...]
        for level, column in enumerate(gates):
            out = jnp.where(table_lane == level * heads + h, column, out)
        gate_grads[...] = out

    def collect(i, h):
        top = i + 1 == bits
        if top:
            @pl.when(uppers[i] == 0)
            def _():
                back_copy(i, h).wait_recv()
                block[h] = block[h] + inbox[i, h]
        else:
            back_copy(i, h).wait_recv()
            block[h] = block[h] + inbox[i, h]
        if i:
            low_level = i - 1
            current = block[h]
            is_upper = above(low_level, square)
            own_keep = meta[bits + low_level][0:1]
            partner_keep = meta[2 * bits + low_level][0:1]
            outbox[low_level, h] = jnp.where(is_upper, current * own_keep + sg[low_level, h], current)
            block[h] = jnp.where(is_upper, current, current * partner_keep)
            back_copy(low_level, h).start()
        else:
            finish(h)

    def finish(h):
        current = block[h]
        first = current * (1.0 - reset_of(off_ref, 1)[0:1]) + low[h]
        kk, vv = k_ref[:, lanes(h)], v_ref[:, lanes(h)]
        for j, state in enumerate((first, current)):
            rows = slice(j * STRETCH, (j + 1) * STRETCH)
            sh, sl = split(state)
            kept = kept_of(off_ref, j)
            gk = dot(vv[rows], sh, NT) + dot(vv[rows], sl, NT)
            gv = dot(kk[rows], sh, NN) + dot(kk[rows], sl, NN)
            gk_ref[rows, lanes(h)] = (gk_part[h, rows] + kept * gk).astype(bf16)
            gv_ref[rows, lanes(h)] = (gv_part[h, rows] + kept * gv).astype(bf16)

    def prepare_gates():
        x = dot(feat_ref[...], w_ref[...], NT)
        logits[...] = jnp.maximum(x, 0.0) + jnp.log1p(jnp.exp(-jnp.abs(x)))
        gate_grads[...] = jnp.zeros(gate_grads.shape, f32)
        slopes[...] = 1.0 / (1.0 + jnp.exp(-x))

    def reduce_gates():
        rows, width = terms.shape[1:]
        dh, dl = split((gate_grads[...] * slopes[...])[:, :rows])
        for n in range(count):
            part = feat_ref[:, n * width : (n + 1) * width]
            terms[n] = dot(dh, part, TN) + dot(dl, part, TN)
        for r in range(1, count):
            term_copy(r).start()

    stages = [make_tail]
    for i in range(bits):
        stages.append(functools.partial(combine, i))
    stages[-1] = lambda h: (combine(bits - 1, h), local_passes(h))
    for i in reversed(range(bits)):
        stages.append(functools.partial(collect, i))
    lag = 2
    passes_at = lag * bits

    def step(wave, carry):
        for depth, stage in enumerate(stages):
            h = wave - depth * lag

            @pl.when((h >= 0) & (h < heads))
            def _():
                stage(h)

            if depth == 0:
                @pl.when(wave == 1)
                def _():
                    set_meta()
                    prepare_gates()
            if depth == bits:
                @pl.when(wave == passes_at + heads - 1)
                def _():
                    reduce_gates()
        return carry

    lax.fori_loop(0, heads + lag * (len(stages) - 1), step, 0)
    total = terms[me]
    for r in range(1, count):
        term_copy(r).wait_recv()
        total = total + got_terms[r - 1]
    for i in range(group_bits):
        sums[i] = total
        sum_copy(i).start()
        sum_copy(i).wait_recv()
        total = sums[i] + got_sums[i]
    gl_out[...] = total

    def drain(h, carry):
        @pl.when(shares(h))
        def _():
            for r in range(1, half):
                share_copy(h, r).wait_send()

        @pl.when(is_low & (lax.rem(h, half) != place))
        def _():
            share_copy(h, 1).wait_recv()

        @pl.when(sends_top(h))
        def _():
            copy(bits - 1, h).wait_send()

        for i in range(bits):
            if i + 1 < bits:
                copy(i, h).wait_send()
                back_copy(i, h).wait_send()
            else:
                @pl.when(uppers[i] == 1)
                def _():
                    back_copy(i, h).wait_send()
        return carry

    lax.fori_loop(0, heads, drain, 0)
    for r in range(1, count):
        flag_copy(r, me).wait_send()
        term_copy(r).wait_send()
    for i in range(group_bits):
        sum_copy(i).wait_send()


def body(queries, key_vectors, value_vectors, features, w_level, offsets, cotangent, final_grad):
    count = lax.axis_size("seq")
    groups = lax.axis_size("dp")
    bits = count.bit_length() - 1
    group_bits = groups.bit_length() - 1
    used = bits + 2
    model = features.shape[-1]
    heads = queries.shape[-1] // HEAD_DIM
    length = queries.shape[1]
    q, k, v, g, feat = queries[0], key_vectors[0], value_vectors[0], cotangent[0], features[0]
    vmem = pl.BlockSpec(memory_space=pltpu.VMEM)
    smem = pl.BlockSpec(memory_space=pltpu.SMEM)
    state = (heads, HEAD_DIM, HEAD_DIM)
    sds = jax.ShapeDtypeStruct
    sem = pltpu.SemaphoreType.DMA
    flat = sds((length, heads * HEAD_DIM), bf16)
    rows = -(-used * heads // 8) * 8
    slab = (rows, model // count)
    table = pltpu.VMEM((length, w_level.shape[1]), f32)
    many = pltpu.VMEM((bits,) + state, f32)
    single = pltpu.VMEM(state, f32)
    part = pltpu.VMEM((heads, length, HEAD_DIM), f32)
    steps = max(group_bits, 1)
    normed, gq, gk, gv, final_state, gl = pl.pallas_call(
        functools.partial(fused_kernel, bits, group_bits, used),
        out_shape=(flat, flat, flat, flat, sds(state, f32), sds(slab, f32)),
        in_specs=[smem] + [vmem] * 7,
        out_specs=(vmem,) * 6,
        scratch_shapes=[
            many, many, single,
            pltpu.VMEM((8, HEAD_DIM), f32),
            pltpu.VMEM((count, 8, HEAD_DIM), f32),
            pltpu.VMEM((4 * bits, 8, HEAD_DIM), f32),
            table, table, table, part, part,
            many, single, single, many, many,
            pltpu.VMEM((count,) + slab, f32),
            pltpu.VMEM((count - 1,) + slab, f32),
            pltpu.VMEM((steps,) + slab, f32),
            pltpu.VMEM((steps,) + slab, f32),
            sem((count - 1,)), sem((count - 1,)),
            sem((bits, heads)), sem((bits, heads)), sem((bits, heads)), sem((bits, heads)),
            sem((count - 1,)), sem((count - 1,)), sem((steps,)), sem((steps,)),
            sem((heads, count // 2 - 1)), sem((heads,)),
        ],
        compiler_params=pltpu.CompilerParams(collective_id=0, has_side_effects=True, vmem_limit_bytes=62 * 1024 * 1024),
        name="fused_layer",
    )(offsets, q, k, v, g, feat, w_level.T, final_grad[0])
    grad_level = jnp.pad(gl[: used * heads].T, ((0, 0), (0, (LEVELS - used) * heads)))
    return normed[None], gq[None], gk[None], gv[None], grad_level, final_state[None]


def solution(mesh):
    in_specs = (
        P("dp", "seq", None),
        P("dp", "seq", None),
        P("dp", "seq", None),
        P("dp", "seq", None),
        P(),
        P("dp", "seq"),
        P("dp", "seq", None),
        P("dp", None, None, None),
    )
    out_specs = (
        P("dp", "seq", None),
        P("dp", "seq", None),
        P("dp", "seq", None),
        P("dp", "seq", None),
        P("seq", None),
        P("dp", None, None, None),
    )
    return jax.shard_map(body, mesh=mesh, in_specs=in_specs, out_specs=out_specs, check_vma=False)
```

```python
import functools

import jax
import jax.numpy as jnp
from jax import lax
from jax.experimental import pallas as pl
from jax.experimental.pallas import tpu as pltpu
from jax.sharding import PartitionSpec as P

HEADS = 12
HEAD_DIM = 128
STRETCH = 128
LEVELS = 12

epsilon = 1e-06
state_scale = 0.0625
f32 = jnp.float32
bf16 = jnp.bfloat16


def split(x):
    hi = x.astype(bf16)
    return hi, (x - hi.astype(f32)).astype(bf16)


def dot(a, b, dims):
    return lax.dot_general(a, b, (dims, ((), ())), preferred_element_type=f32)


NN = ((1,), (0,))
NT = ((1,), (1,))
TN = ((0,), (0,))


def bit_of(index, i):
    return lax.rem(index // (1 << i), 2)


def partner_of(index, i):
    return index + (1 << i) * (1 - 2 * bit_of(index, i))


def greet(targets):
    barrier = pltpu.get_barrier_semaphore()
    for target in targets:
        pl.semaphore_signal(barrier, inc=1, device_id=target, device_id_type=pl.DeviceIdType.MESH)
    pl.semaphore_wait(barrier, len(targets))


def remote(src, dst, send_sem, recv_sem, target):
    return pltpu.make_async_remote_copy(
        src_ref=src,
        dst_ref=dst,
        send_sem=send_sem,
        recv_sem=recv_sem,
        device_id=target,
        device_id_type=pl.DeviceIdType.MESH,
    )


def columns(h):
    return slice(h * HEAD_DIM, (h + 1) * HEAD_DIM)


def offset_plane(off_ref, j, shape):
    return jnp.full(shape, off_ref[0, j], jnp.int32)


def kept_of(off_ref, j):
    off = offset_plane(off_ref, j, (STRETCH, HEAD_DIM))
    position = lax.broadcasted_iota(jnp.int32, (STRETCH, HEAD_DIM), 0)
    return jnp.where((off >= STRETCH) | (position >= off), 1.0, 0.0).astype(f32)


def reset_of(off_ref, j):
    return jnp.where(offset_plane(off_ref, j, (8, HEAD_DIM)) < STRETCH, 1.0, 0.0).astype(f32)


def fused_kernel(bits, group_bits, used, off_ref, q_ref, k_ref, v_ref, g_ref, feat_ref, w_ref, fin_ref,
                 normed_ref, gq_ref, gk_ref, gv_ref, final_ref, gl_out,
                 own, states, tails, own_flag, all_flags, meta, logits, slopes, gate_grads, gk_part, gv_part,
                 sg, low, block, outbox, inbox, terms, half_in, merged, got_terms, sums, got_sums,
                 fsend, frecv, send, recv, bsend, brecv, tsend, trecv, ssend, srecv, hsend, hrecv, xsend, xrecv):
    me = lax.axis_index("seq")
    group = lax.axis_index("dp")
    count = 1 << bits
    heads = block.shape[0]
    partners = [{"seq": partner_of(me, i)} for i in range(bits)]
    uppers = [bit_of(me, i) for i in range(bits)]
    peers = [{"seq": lax.rem(me + r, count)} for r in range(1, count)]
    siblings = [{"dp": partner_of(group, i)} for i in range(group_bits)]
    square = (HEAD_DIM, HEAD_DIM)
    greet(peers + siblings)

    def lanes(h):
        return pl.ds(pl.multiple_of(h * HEAD_DIM, HEAD_DIM), HEAD_DIM)

    def flag_copy(r, owner):
        return remote(own_flag, all_flags.at[owner], fsend.at[r - 1], frecv.at[r - 1], peers[r - 1])

    def copy(i, h):
        return remote(own.at[i, h], states.at[i, h], send.at[i, h], recv.at[i, h], partners[i])

    def back_copy(i, h):
        return remote(outbox.at[i, h], inbox.at[i, h], bsend.at[i, h], brecv.at[i, h], partners[i])

    def term_copy(r):
        return remote(merged.at[lax.rem(me + r, count)], got_terms.at[r - 1], tsend.at[r - 1], trecv.at[r - 1], peers[r - 1])

    def sum_copy(i):
        return remote(sums.at[i], got_sums.at[i], ssend.at[i], srecv.at[i], siblings[i])

    half = count // 2
    place = lax.rem(me, half)
    is_low = uppers[bits - 1] == 0
    mates = [{"seq": me - place + lax.rem(place + r, half)} for r in range(1, half)]

    def leads(h):
        return lax.rem(h, half) == place

    def shares(h):
        return is_low & leads(h)

    def sends_top(h):
        return is_low | leads(h)

    def share_copy(h, r):
        return remote(final_ref.at[h], final_ref.at[h], hsend.at[h, r - 1], hrecv.at[h], mates[r - 1])

    side = bit_of(group, 0)

    def half_copy():
        return remote(terms.at[1 - side], half_in, xsend.at[0], xrecv.at[0], siblings[0])

    def result_copy(which):
        return remote(gl_out.at[which], gl_out.at[which], xsend.at[1], xrecv.at[1], siblings[0])

    def above(i, shape):
        return jnp.full(shape, uppers[i], jnp.int32) > 0

    own_flag[...] = jnp.maximum(reset_of(off_ref, 0), reset_of(off_ref, 1))
    all_flags[me] = own_flag[...]
    for r in range(1, count):
        flag_copy(r, me).start()

    def set_meta():
        for r in range(1, count):
            flag_copy(r, lax.rem(me - r + count, count)).wait_recv()
        prefix = jnp.zeros((8, HEAD_DIM), f32)
        for i in range(bits):
            base = (me // (1 << i)) * (1 << i)
            other = base + (1 << i) * (1 - 2 * uppers[i])
            mine, theirs = all_flags[base], all_flags[other]
            for j in range(1, 1 << i):
                mine = jnp.maximum(mine, all_flags[base + j])
                theirs = jnp.maximum(theirs, all_flags[other + j])
            is_upper = above(i, (8, HEAD_DIM))
            meta[i] = is_upper.astype(f32) * (1.0 - prefix)
            meta[bits + i] = 1.0 - mine
            meta[2 * bits + i] = 1.0 - theirs
            meta[3 * bits + i] = jnp.where(is_upper, mine, theirs)
            prefix = jnp.where(is_upper, jnp.maximum(prefix, theirs), prefix)

    def make_tail(h):
        kk, vv = k_ref[:, lanes(h)], v_ref[:, lanes(h)]
        tail = []
        for j in range(2):
            rows = slice(j * STRETCH, (j + 1) * STRETCH)
            tail.append(dot(kk[rows] * kept_of(off_ref, j).astype(bf16), vv[rows], TN))
        tails[h] = tail[0]
        own[0, h] = jnp.where(reset_of(off_ref, 1)[0:1] > 0.5, tail[1], tail[0] + tail[1])
        copy(0, h).start()

    def combine(i, h):
        def joined():
            mine, theirs = own[i, h], states[i, h]
            drop = meta[3 * bits + i][0:1] > 0.5
            return jnp.where(drop, jnp.where(above(i, square), mine, theirs), mine + theirs)

        if i + 1 < bits:
            copy(i, h).wait_recv()
            own[i + 1, h] = joined()
            if i + 2 < bits:
                copy(i + 1, h).start()
            else:
                @pl.when(sends_top(h))
                def _():
                    copy(i + 1, h).start()
        else:
            @pl.when((uppers[i] == 1) | leads(h))
            def _():
                copy(i, h).wait_recv()
                final_ref[h] = joined() * state_scale

            @pl.when(shares(h))
            def _():
                for r in range(1, half):
                    share_copy(h, r).start()

    def local_passes(h):
        position = lax.broadcasted_iota(jnp.int32, (STRETCH, HEAD_DIM), 0)
        source = lax.broadcasted_iota(jnp.int32, (STRETCH, STRETCH), 1)
        table = logits[...]
        table_lane = lax.broadcasted_iota(jnp.int32, table.shape, 1)

        def gate_of(level):
            x = jnp.sum(jnp.where(table_lane == level * heads + h, table, 0.0), -1, keepdims=True)
            return x

        gate = [gate_of(level) for level in range(used)]
        reset_low = reset_of(off_ref, 0)[0:1]
        q, k, v = q_ref[:, lanes(h)], k_ref[:, lanes(h)], v_ref[:, lanes(h)]
        halves = (slice(0, STRETCH), slice(STRETCH, 2 * STRETCH))
        opens, alloweds, scores, gated, weights, intra = [], [], [], [], [], []
        for j, rows in enumerate(halves):
            off = offset_plane(off_ref, j, (STRETCH, HEAD_DIM))
            after = position >= off
            opens.append(jnp.where(after, 0.0, 1.0).astype(f32))
            allowed = jnp.where((position >= source) & jnp.logical_not(after & (source < off)), 1.0, 0.0).astype(f32)
            alloweds.append(allowed)
            scores.append(dot(q[rows], k[rows], NT))
            gated.append(allowed * gate[0][rows])
            weights.append(split(scores[j] * gated[j]))
            wh, wl = weights[j]
            intra.append(dot(wh, v[rows], NN) + dot(wl, v[rows], NN))
        open_all = jnp.concatenate(opens, 0)
        near_h, near_l = split(tails[h])
        near_out = dot(q[STRETCH:], near_h, NN) + dot(q[STRETCH:], near_l, NN)
        near_scale = gate[1][STRETCH:] * opens[1]
        intra[1] = intra[1] + near_scale * near_out
        mixed = jnp.concatenate(intra, 0)
        ok = jnp.concatenate([jnp.ones((STRETCH, HEAD_DIM), f32), jnp.zeros((STRETCH, HEAD_DIM), f32) + (1.0 - reset_low)], 0)
        masks, products, pieces = [], [], []
        for i in range(bits):
            sh, sl = split(states[i, h])
            pieces.append((sh, sl))
            product = dot(q, sh, NN) + dot(q, sl, NN)
            mask = open_all * ok * meta[i][0:1]
            masks.append(mask)
            products.append(product)
            mixed = mixed + gate[2 + i] * mask * product
        r = lax.rsqrt(jnp.mean(mixed * mixed, -1, keepdims=True) + epsilon)
        normed = mixed * r
        normed_ref[:, lanes(h)] = normed.astype(bf16)
        g = g_ref[:, lanes(h)].astype(f32)
        gs = r * (g - normed * jnp.mean(g * normed, -1, keepdims=True))
        gh, gl = split(gs)
        gq, gintra = [], []
        for j, rows in enumerate(halves):
            gw = dot(gh[rows], v[rows], NT) + dot(gl[rows], v[rows], NT)
            gintra.append(jnp.sum(gw * alloweds[j] * scores[j], -1, keepdims=True))
            sh, sl = split(gw * gated[j])
            wh, wl = weights[j]
            gv_part[h, rows] = dot(wh, gh[rows], TN) + dot(wh, gl[rows], TN) + dot(wl, gh[rows], TN)
            gk_part[h, rows] = dot(sh, q[rows], TN) + dot(sl, q[rows], TN)
            gq.append(dot(sh, k[rows], NN) + dot(sl, k[rows], NN))
        upper = halves[1]
        nh, nl = split(near_scale * gs[upper])
        gq[1] = gq[1] + dot(nh, near_h, NT) + dot(nh, near_l, NT) + dot(nl, near_h, NT)
        low[h] = dot(q[upper], nh, TN) + dot(q[upper], nl, TN)
        gnear = jnp.sum(near_out * gs[upper] * opens[1], -1, keepdims=True)
        gates = [jnp.concatenate(gintra, 0), jnp.concatenate([jnp.zeros((STRETCH, 1), f32), gnear], 0)]
        total = jnp.concatenate(gq, 0)
        for i in reversed(range(bits)):
            sh, sl = pieces[i]
            masked = masks[i] * gs
            gates.insert(2, jnp.sum(products[i] * masked, -1, keepdims=True))
            wh, wl = split(gate[2 + i] * masked)
            state_grad = dot(q, wh, TN) + dot(q, wl, TN)
            if i + 1 == bits:
                outbox[i, h] = state_grad
                grad = fin_ref[h].astype(f32) * state_scale
                first = jnp.full(square, lax.rem(me, count // 2), jnp.int32) == 0
                keep = jnp.where(above(i, square), 1.0, meta[2 * bits + i][0:1])
                block[h] = jnp.where(first, grad, 0.0) * keep

                @pl.when(uppers[i] == 1)
                def _():
                    back_copy(i, h).start()
            else:
                sg[i, h] = state_grad
            total = total + dot(wh, sh, NT) + dot(wh, sl, NT) + dot(wl, sh, NT)
        gq_ref[:, lanes(h)] = total.astype(bf16)
        out = gate_grads[...]
        for level, column in enumerate(gates):
            out = jnp.where(table_lane == level * heads + h, column, out)
        gate_grads[...] = out

    def collect(i, h):
        top = i + 1 == bits
        if top:
            @pl.when(uppers[i] == 0)
            def _():
                back_copy(i, h).wait_recv()
                block[h] = block[h] + inbox[i, h]
        else:
            back_copy(i, h).wait_recv()
            block[h] = block[h] + inbox[i, h]
        if i:
            low_level = i - 1
            current = block[h]
            is_upper = above(low_level, square)
            own_keep = meta[bits + low_level][0:1]
            partner_keep = meta[2 * bits + low_level][0:1]
            outbox[low_level, h] = jnp.where(is_upper, current * own_keep + sg[low_level, h], current)
            block[h] = jnp.where(is_upper, current, current * partner_keep)
            back_copy(low_level, h).start()
        else:
            finish(h)

    def finish(h):
        current = block[h]
        first = current * (1.0 - reset_of(off_ref, 1)[0:1]) + low[h]
        kk, vv = k_ref[:, lanes(h)], v_ref[:, lanes(h)]
        for j, state in enumerate((first, current)):
            rows = slice(j * STRETCH, (j + 1) * STRETCH)
            sh, sl = split(state)
            kept = kept_of(off_ref, j)
            gk = dot(vv[rows], sh, NT) + dot(vv[rows], sl, NT)
            gv = dot(kk[rows], sh, NN) + dot(kk[rows], sl, NN)
            gk_ref[rows, lanes(h)] = (gk_part[h, rows] + kept * gk).astype(bf16)
            gv_ref[rows, lanes(h)] = (gv_part[h, rows] + kept * gv).astype(bf16)

    def prepare_gates():
        x = dot(feat_ref[...], w_ref[...], NT)
        logits[...] = jnp.maximum(x, 0.0) + jnp.log1p(jnp.exp(-jnp.abs(x)))
        gate_grads[...] = jnp.zeros(gate_grads.shape, f32)
        slopes[...] = 1.0 / (1.0 + jnp.exp(-x))

    def reduce_gates():
        rows, width = terms.shape[2:]
        dh, dl = split((gate_grads[...] * slopes[...])[:, : 2 * rows])
        for n in range(count):
            part = feat_ref[:, n * width : (n + 1) * width]
            product = dot(dh, part, TN) + dot(dl, part, TN)
            terms[0, n] = product[:rows]
            terms[1, n] = product[rows:]
        half_copy().start()

    def merge_gates():
        half_copy().wait_recv()
        for n in range(count):
            merged[n] = terms[side, n] + half_in[n]
        for r in range(1, count):
            term_copy(r).start()

    stages = [make_tail]
    for i in range(bits):
        stages.append(functools.partial(combine, i))
    stages[-1] = lambda h: (combine(bits - 1, h), local_passes(h))
    for i in reversed(range(bits)):
        stages.append(functools.partial(collect, i))
    lag = 2
    passes_at = lag * bits

    def step(wave, carry):
        for depth, stage in enumerate(stages):
            h = wave - depth * lag

            @pl.when((h >= 0) & (h < heads))
            def _():
                stage(h)

            if depth == 0:
                @pl.when(wave == 1)
                def _():
                    set_meta()
                    prepare_gates()
            if depth == bits:
                @pl.when(wave == passes_at + heads - 1)
                def _():
                    reduce_gates()

                @pl.when(wave == passes_at + heads)
                def _():
                    merge_gates()
        return carry

    lax.fori_loop(0, heads + lag * (len(stages) - 1), step, 0)
    total = merged[me]
    for r in range(1, count):
        term_copy(r).wait_recv()
        total = total + got_terms[r - 1]
    for i in range(1, group_bits):
        sums[i] = total
        sum_copy(i).start()
        sum_copy(i).wait_recv()
        total = sums[i] + got_sums[i]
    gl_out[side] = total
    result_copy(side).start()

    def drain(h, carry):
        @pl.when(shares(h))
        def _():
            for r in range(1, half):
                share_copy(h, r).wait_send()

        @pl.when(is_low & (lax.rem(h, half) != place))
        def _():
            share_copy(h, 1).wait_recv()

        @pl.when(sends_top(h))
        def _():
            copy(bits - 1, h).wait_send()

        for i in range(bits):
            if i + 1 < bits:
                copy(i, h).wait_send()
                back_copy(i, h).wait_send()
            else:
                @pl.when(uppers[i] == 1)
                def _():
                    back_copy(i, h).wait_send()
        return carry

    lax.fori_loop(0, heads, drain, 0)
    for r in range(1, count):
        flag_copy(r, me).wait_send()
        term_copy(r).wait_send()
    for i in range(1, group_bits):
        sum_copy(i).wait_send()
    half_copy().wait_send()
    result_copy(side).wait_send()
    result_copy(1 - side).wait_recv()


def body(queries, key_vectors, value_vectors, features, w_level, offsets, cotangent, final_grad):
    count = lax.axis_size("seq")
    groups = lax.axis_size("dp")
    bits = count.bit_length() - 1
    group_bits = groups.bit_length() - 1
    used = bits + 2
    model = features.shape[-1]
    heads = queries.shape[-1] // HEAD_DIM
    length = queries.shape[1]
    q, k, v, g, feat = queries[0], key_vectors[0], value_vectors[0], cotangent[0], features[0]
    vmem = pl.BlockSpec(memory_space=pltpu.VMEM)
    smem = pl.BlockSpec(memory_space=pltpu.SMEM)
    state = (heads, HEAD_DIM, HEAD_DIM)
    sds = jax.ShapeDtypeStruct
    sem = pltpu.SemaphoreType.DMA
    flat = sds((length, heads * HEAD_DIM), bf16)
    rows = -(-used * heads // 16) * 8
    slab = (rows, model // count)
    table = pltpu.VMEM((length, w_level.shape[1]), f32)
    many = pltpu.VMEM((bits,) + state, f32)
    single = pltpu.VMEM(state, f32)
    part = pltpu.VMEM((heads, length, HEAD_DIM), f32)
    steps = max(group_bits, 1)
    normed, gq, gk, gv, final_state, gl = pl.pallas_call(
        functools.partial(fused_kernel, bits, group_bits, used),
        out_shape=(flat, flat, flat, flat, sds(state, f32), sds((2,) + slab, f32)),
        in_specs=[smem] + [vmem] * 7,
        out_specs=(vmem,) * 6,
        scratch_shapes=[
            many, many, single,
            pltpu.VMEM((8, HEAD_DIM), f32),
            pltpu.VMEM((count, 8, HEAD_DIM), f32),
            pltpu.VMEM((4 * bits, 8, HEAD_DIM), f32),
            table, table, table, part, part,
            many, single, single, many, many,
            pltpu.VMEM((2, count) + slab, f32),
            pltpu.VMEM((count,) + slab, f32),
            pltpu.VMEM((count,) + slab, f32),
            pltpu.VMEM((count - 1,) + slab, f32),
            pltpu.VMEM((steps,) + slab, f32),
            pltpu.VMEM((steps,) + slab, f32),
            sem((count - 1,)), sem((count - 1,)),
            sem((bits, heads)), sem((bits, heads)), sem((bits, heads)), sem((bits, heads)),
            sem((count - 1,)), sem((count - 1,)), sem((steps,)), sem((steps,)),
            sem((heads, count // 2 - 1)), sem((heads,)), sem((2,)), sem((2,)),
        ],
        compiler_params=pltpu.CompilerParams(collective_id=0, has_side_effects=True, vmem_limit_bytes=62 * 1024 * 1024),
        name="fused_layer",
    )(offsets, q, k, v, g, feat, w_level.T, final_grad[0])
    grad_level = jnp.pad(gl.reshape(2 * rows, slab[1])[: used * heads].T, ((0, 0), (0, (LEVELS - used) * heads)))
    return normed[None], gq[None], gk[None], gv[None], grad_level, final_state[None]


def solution(mesh):
    in_specs = (
        P("dp", "seq", None),
        P("dp", "seq", None),
        P("dp", "seq", None),
        P("dp", "seq", None),
        P(),
        P("dp", "seq"),
        P("dp", "seq", None),
        P("dp", None, None, None),
    )
    out_specs = (
        P("dp", "seq", None),
        P("dp", "seq", None),
        P("dp", "seq", None),
        P("dp", "seq", None),
        P("seq", None),
        P("dp", None, None, None),
    )
    return jax.shard_map(body, mesh=mesh, in_specs=in_specs, out_specs=out_specs, check_vma=False)
```
